1024 devices in a mesh: sub: 8 (over z_lo, core), lat: 128 (over x, z_hi, y).
Axes of the slice: x: 4, y: 8, z: 16 (z_hi: 4, z_lo: 4; z = z_hi * 4 + z_lo), core: 2. Of those that a mesh axis runs over, the one named last changes fastest.
Arguments:
- sources: float32 [8, 24, 524288], P(None, None, ('sub', 'lat')), may hold values from -6 to 6
- guess: float32 [8, 24, 524288], P(None, None, ('sub', 'lat')), may hold values from -6 to 6
- links: float32 [4, 18, 524288], P(None, None, ('sub', 'lat')), may hold values from -1 to 1, as said below
Outputs:
- solution: float32 [8, 24, 524288], P(None, None, ('sub', 'lat'))
The draws below stay inside these ranges and needn't reach their ends.
Inputs may be any that keep to these rules, and one draw needn't show every extreme that they name: `links`: for each direction and site the 18 numbers are a 3 x 3 complex matrix (row, column, real and imaginary part) that is special unitary.
All inputs are finite; a program needn't handle non-finite values.
Results may differ from the reference program's by a relative error of at most 0.00002.
Values sent between devices are 32-bit elements; how exact they have to be, the bound alone decides.
A program may use at most 128 MiB of HBM per device.

```python
import jax
import jax.numpy as jnp
from jax import lax

TB = 2
BZ = 2
BY = 4
LX = 32
ITERS = 2
QY = 8
SOURCES = 8
LT = 16
LZ = 32
LY = 32
N_SUB = 8


def complex_times(left_real, left_imag, right_real, right_imag):
    return (left_real * right_real - left_imag * right_imag, left_real * right_imag + left_imag * right_real)


def draw_links(key, part):
    samples = jax.random.normal(jax.random.fold_in(key, 17), (4, 2, 2, 3, LT * LZ * LY * LX), jnp.float32)
    first_real = samples[:, 0, 0]
    first_imag = samples[:, 0, 1]
    second_real = samples[:, 1, 0]
    second_imag = samples[:, 1, 1]
    scale_first = jnp.sqrt(jnp.sum(first_real * first_real + first_imag * first_imag, axis=1, keepdims=True)) + 1e-06
    zero_real = first_real / scale_first
    zero_imag = first_imag / scale_first
    intersection_real = jnp.sum(zero_real * second_real + zero_imag * second_imag, axis=1, keepdims=True)
    intersection_imag = jnp.sum(zero_real * second_imag - zero_imag * second_real, axis=1, keepdims=True)
    along_real, along_imag = complex_times(intersection_real, intersection_imag, zero_real, zero_imag)
    remain_real = second_real - along_real
    remain_imag = second_imag - along_imag
    scale_second = jnp.sqrt(jnp.sum(remain_real * remain_real + remain_imag * remain_imag, axis=1, keepdims=True)) + 1e-06
    one_real = remain_real / scale_second
    one_imag = remain_imag / scale_second
    third_real = []
    third_imag = []
    for target in range(3):
        before_index = (target + 1) % 3
        after_index = (target + 2) % 3
        cross_real_first, cross_imag_first = complex_times(zero_real[:, before_index], zero_imag[:, before_index], one_real[:, after_index], one_imag[:, after_index])
        cross_real_second, cross_imag_second = complex_times(zero_real[:, after_index], zero_imag[:, after_index], one_real[:, before_index], one_imag[:, before_index])
        third_real.append(cross_real_first - cross_real_second)
        third_imag.append(cross_imag_second - cross_imag_first)
    row_zero = jnp.stack([zero_real, zero_imag], axis=2)
    row_one = jnp.stack([one_real, one_imag], axis=2)
    row_two = jnp.stack([jnp.stack(third_real, axis=1), jnp.stack(third_imag, axis=1)], axis=2)
    matrix = jnp.stack([row_zero, row_one, row_two], axis=1)
    return matrix.reshape((4, 18, LT * LZ * LY * LX))


def levels(key, shape, cuts, least, largest):
    gain, own = 1.0, jax.random.fold_in(key, 6)
    for position, shards_of in cuts:
        draws = jnp.exp(jax.random.uniform(jax.random.fold_in(own, position), (shards_of,), jnp.float32, least / len(cuts), largest / len(cuts)))
        gain = gain * jnp.repeat(draws, shape[position] // shards_of).reshape([-1 if axis == position else 1 for axis in range(len(shape))])
    return gain


def bell_draw(stream_key, dims, scale, most, cuts=(), kind=jnp.bfloat16):
    factor_of = levels(stream_key, dims, cuts, -0.22, 0.18) if cuts else 1.0
    drawn = jax.random.normal(stream_key, dims, jnp.float32) * scale * factor_of
    return jnp.minimum(jnp.maximum(drawn, -most), most).astype(kind)


def setup_inputs(seed: int = 0) -> dict:
    seeds = jax.random.split(jax.random.key(seed), 4)
    sources = bell_draw(seeds[0], (SOURCES, 24, LT * LZ * LY * LX), 1.0, 6.0, ((2, 1024),), jnp.float32)
    guess = bell_draw(seeds[1], (SOURCES, 24, LT * LZ * LY * LX), 1.0, 6.0, ((2, 1024),), jnp.float32)
    links = draw_links(jax.random.fold_in(seeds[3], 71), 0)
    return dict(sources=sources, guess=guess, links=links)


HOPPING = 0.125
RELAXATION = 1.0

UPPER_BLOCKS = (
    (((0, 0), (1.0, 0.0)), ((1, 1), (1.0, 0.0))),
    (((0, 0), (0.0, 1.0)), ((1, 1), (0.0, -1.0))),
    (((0, 1), (-1.0, 0.0)), ((1, 0), (1.0, 0.0))),
    (((0, 1), (0.0, 1.0)), ((1, 0), (0.0, 1.0))),
)
LOWER_BLOCKS = (
    (((0, 0), (1.0, 0.0)), ((1, 1), (1.0, 0.0))),
    (((0, 0), (0.0, -1.0)), ((1, 1), (0.0, 1.0))),
    (((0, 1), (1.0, 0.0)), ((1, 0), (-1.0, 0.0))),
    (((0, 1), (0.0, -1.0)), ((1, 0), (0.0, -1.0))),
)


def scaled(factor, spinor):
    real_part = spinor[:, :, 0]
    imag_part = spinor[:, :, 1]
    return jnp.stack([factor[0] * real_part - factor[1] * imag_part, factor[0] * imag_part + factor[1] * real_part], axis=2)


def apply_block(entries, first_spin, second_spin):
    pieces = [first_spin, second_spin]
    outputs = [None, None]
    for (target, source), factor in entries:
        outputs[target] = scaled(factor, pieces[source])
    return outputs


def project(field, direction, parity):
    coupled = apply_block(UPPER_BLOCKS[direction], field[:, 2], field[:, 3])
    return jnp.stack([field[:, 0] - parity * coupled[0], field[:, 1] - parity * coupled[1]], axis=1)


def rebuild(halves, direction, parity):
    coupled = apply_block(LOWER_BLOCKS[direction], halves[:, 0], halves[:, 1])
    return jnp.concatenate([halves, jnp.stack([-parity * coupled[0], -parity * coupled[1]], axis=1)], axis=1)


def color_product(matrix, halves, adjoint):
    row_list = []
    for target in range(3):
        real_sum = 0.0
        imag_sum = 0.0
        for source in range(3):
            if adjoint:
                entry_real = matrix[source, target, 0]
                entry_imag = -matrix[source, target, 1]
            else:
                entry_real = matrix[target, source, 0]
                entry_imag = matrix[target, source, 1]
            vector_real = halves[:, :, source, 0]
            vector_imag = halves[:, :, source, 1]
            real_sum = real_sum + entry_real * vector_real - entry_imag * vector_imag
            imag_sum = imag_sum + entry_real * vector_imag + entry_imag * vector_real
        row_list.append(jnp.stack([real_sum, imag_sum], axis=2))
    return jnp.stack(row_list, axis=2)


def neighbour(halves, direction, forward):
    lattice_axis = 4 + direction
    shifted = jnp.roll(halves, -1 if forward else 1, lattice_axis)
    if direction == 0:
        length = halves.shape[4]
        edge_index = length - 1 if forward else 0
        sign_flip = jnp.where(jnp.arange(length) == edge_index, -1.0, 1.0).astype(halves.dtype)
        shifted = shifted * sign_flip.reshape((length, 1, 1, 1))
    return shifted


def hopping_terms(field, links):
    hop_total = jnp.zeros_like(field)
    for direction in range(4):
        matrix = links[direction]
        ahead = neighbour(project(field, direction, 1.0), direction, True)
        hop_total = hop_total + rebuild(color_product(matrix, ahead, False), direction, 1.0)
        behind = neighbour(color_product(matrix, project(field, direction, -1.0), True), direction, False)
        hop_total = hop_total + rebuild(behind, direction, -1.0)
    return hop_total


def wilson(field, links):
    return field - HOPPING * hopping_terms(field, links)


def natural(array, lead_shape):
    count = len(lead_shape)
    shaped = array.reshape(lead_shape + (N_SUB, LZ // BZ, QY, TB, BZ, BY, LX))
    order = list(range(count)) + [count + k for k in (0, 3, 1, 4, 2, 5, 6)]
    return jnp.transpose(shaped, order).reshape(lead_shape + (LT, LZ, LY, LX))


def stored(array, lead_shape, final_shape):
    count = len(lead_shape)
    shaped = array.reshape(lead_shape + (N_SUB, TB, LZ // BZ, BZ, QY, BY, LX))
    order = list(range(count)) + [count + k for k in (0, 2, 4, 1, 3, 5, 6)]
    return jnp.transpose(shaped, order).reshape(final_shape)


def reference(sources, guess, links):
    spinor_lead = (SOURCES, 4, 3, 2)
    source_field = natural(sources, spinor_lead)
    guess_field = natural(guess, spinor_lead)
    link_field = natural(links, (4, 3, 3, 2))

    def solve_source(members):
        source_one = members[0][None]
        guess_one = members[1][None]
        residual = source_one - wilson(guess_one, link_field)
        solution = guess_one
        for iteration in range(ITERS):
            solution = solution + RELAXATION * residual
            if iteration + 1 < ITERS:
                residual = residual - RELAXATION * wilson(residual, link_field)
        return solution[0]

    solved = lax.map(solve_source, (source_field, guess_field))
    return stored(solved, spinor_lead, sources.shape)
```

```python
import functools

import jax
import jax.numpy as jnp
from jax import lax
from jax.experimental import pallas as pl
from jax.experimental.pallas import tpu as pltpu
from jax.sharding import PartitionSpec as P

HOPPING = 0.125
MESH = pl.DeviceIdType.MESH
F32 = jnp.float32
ROW = 32
LANES = 128

UPPER = (
    ((0, 0), (1, 0)),
    ((0, 1), (1, 3)),
    ((1, 2), (0, 0)),
    ((1, 1), (0, 1)),
)
LOWER = (
    ((0, 0), (1, 0)),
    ((0, 3), (1, 1)),
    ((1, 0), (0, 2)),
    ((1, 3), (0, 3)),
)


def turned(pair, power):
    re, im = pair
    return (
        ((1, re), (1, im)),
        ((-1, im), (1, re)),
        ((-1, re), (-1, im)),
        ((1, im), (-1, re)),
    )[power]


def plus(value, sign, other):
    return value + other if sign > 0 else value - other


def project(f, m, parity):
    result = []
    for spin in range(2):
        half, power = UPPER[m][spin]
        for color in range(3):
            base = (spin * 3 + color) * 2
            low = ((2 + half) * 3 + color) * 2
            parts = turned((f[low], f[low + 1]), power)
            for part in range(2):
                sign, value = parts[part]
                result.append(plus(f[base + part], -parity * sign, value))
    return result


def add_rebuilt(total, h, m, parity):
    result = []
    for index in range(12):
        result.append(h[index] if total is None else total[index] + h[index])
    for spin in range(2):
        half, power = LOWER[m][spin]
        for color in range(3):
            low = (half * 3 + color) * 2
            parts = turned((h[low], h[low + 1]), power)
            for part in range(2):
                sign, value = parts[part]
                sign = -parity * sign
                place = ((2 + spin) * 3 + color) * 2 + part
                if total is None:
                    result.append(value if sign > 0 else -value)
                else:
                    result.append(plus(total[place], sign, value))
    return result


def color_product(u, h, adjoint):
    result = []
    for spin in range(2):
        for target in range(3):
            re = im = None
            for source in range(3):
                entry = (source * 3 + target if adjoint else target * 3 + source) * 2
                ur, ui = u[entry], u[entry + 1]
                vr, vi = h[(spin * 3 + source) * 2], h[(spin * 3 + source) * 2 + 1]
                if re is None:
                    re, im = ur * vr, ur * vi
                else:
                    re, im = re + ur * vr, im + ur * vi
                if adjoint:
                    re, im = re + ui * vi, im - ui * vr
                else:
                    re, im = re - ui * vi, im + ui * vr
            result.append(re)
            result.append(im)
    return result


def roll(value, shift):
    shift = shift % LANES
    return value if shift == 0 else pltpu.roll(value, shift, 1)


def kernel(
    y_blocks, g_hbm, s_hbm, l_hbm, o_hbm, g_v, s_v, l_v, o_v, lb, x1, acc, zf, zb, zr, tf, tb, tr, yf, yb, ys, yr,
    in_sem, out_sem, zs_sem, zr_sem, ts_sem, tr_sem, ys_sem, yr_sem,
):
    sub, lat = lax.axis_index("sub"), lax.axis_index("lat")
    n_sub, n_lat = lax.axis_size("sub"), lax.axis_size("lat")
    row, column = lat // y_blocks, lat % y_blocks
    t_up, t_down = ((sub + 1) % n_sub, lat), ((sub + n_sub - 1) % n_sub, lat)
    z_up, z_down = (sub, (lat + y_blocks) % n_lat), (sub, (lat + n_lat - y_blocks) % n_lat)
    y_up = (sub, row * y_blocks + (column + 1) % y_blocks)
    y_down = (sub, row * y_blocks + (column + y_blocks - 1) % y_blocks)

    barrier = pltpu.get_barrier_semaphore()
    for other in (z_up, z_down, t_up, t_down, y_up, y_down):
        pl.semaphore_signal(barrier, inc=1, device_id=other, device_id_type=MESH)

    def lanes(cell):
        return pl.ds(cell * LANES, LANES)

    loads = [pltpu.make_async_copy(l_hbm, l_v, in_sem.at[8])]
    for cell in range(4):
        loads.append(pltpu.make_async_copy(g_hbm.at[:, lanes(cell)], g_v.at[cell], in_sem.at[cell]))
    for cell in range(4):
        loads.append(pltpu.make_async_copy(s_hbm.at[:, lanes(cell)], s_v.at[cell], in_sem.at[4 + cell]))
    for load in loads:
        load.start()

    place = lax.broadcasted_iota(jnp.int32, (16, LANES), 1)
    x_last, x_first = place % ROW == ROW - 1, place % ROW == 0
    group = place // ROW

    def spread(ref, t, comp):
        rows = pl.ds(comp, 8, stride=24)
        return jnp.concatenate([ref[2 * t, rows, :], ref[2 * t + 1, rows, :]], axis=0)

    def guess_of(t):
        return [spread(g_v, t, comp) for comp in range(24)]

    def first_of(t):
        return [x1[t, comp] for comp in range(24)]

    def link(t, m):
        return [lb[t, m, entry] for entry in range(18)]

    def copy(src, dst, send, recv, other):
        return pltpu.make_async_remote_copy(
            src_ref=src, dst_ref=dst, send_sem=send, recv_sem=recv, device_id=other, device_id_type=MESH
        )

    def z_copies(k, t):
        return [
            copy(zf.at[k, t, 0], zr.at[k, t, 0], zs_sem.at[k, t, 0], zr_sem.at[k, t, 0], z_down),
            copy(zb.at[k, t, 1], zr.at[k, t, 1], zs_sem.at[k, t, 1], zr_sem.at[k, t, 1], z_up),
        ]

    def t_copy(k, t):
        src, other = (tf, t_down) if t == 0 else (tb, t_up)
        return copy(src.at[k, t], tr.at[k, t], ts_sem.at[k, t], tr_sem.at[k, t], other)

    def y_copies(k, t):
        return [
            copy(ys.at[k, t, 0], yr.at[k, t, 0], ys_sem.at[k, t, 0], yr_sem.at[k, t, 0], y_down),
            copy(ys.at[k, t, 1], yr.at[k, t, 1], ys_sem.at[k, t, 1], yr_sem.at[k, t, 1], y_up),
        ]

    def prepare_z(k, t, field):
        f = field(t)
        ahead = project(f, 1, 1)
        behind = color_product(link(t, 1), project(f, 1, -1), True)
        for comp in range(12):
            for z in range(2):
                zf[k, t, z, comp] = ahead[comp][8 * z : 8 * z + 8]
                zb[k, t, z, comp] = behind[comp][8 * z : 8 * z + 8]

    def prepare_t(k, t, field):
        f = field(t)
        ahead = project(f, 0, 1)
        behind = color_product(link(t, 0), project(f, 0, -1), True)
        if t == 0:
            sign = jnp.where(sub == 0, -1.0, 1.0).astype(F32)
            ahead = [value * sign for value in ahead]
        else:
            sign = jnp.where(sub == n_sub - 1, -1.0, 1.0).astype(F32)
            behind = [value * sign for value in behind]
        for comp in range(12):
            tf[k, t, comp] = ahead[comp]
            tb[k, t, comp] = behind[comp]

    def prepare_y(k, t, field):
        f = field(t)
        ahead = project(f, 2, 1)
        behind = color_product(link(t, 2), project(f, 2, -1), True)
        for quad in range(3):
            packed = [None, None]
            for j in range(4):
                comp = 4 * quad + j
                up, down = roll(ahead[comp], -ROW), roll(behind[comp], ROW)
                yf[k, t, comp] = up
                yb[k, t, comp] = down
                up = up if j == 3 else roll(ahead[comp], ROW * j)
                down = down if j == 0 else roll(behind[comp], ROW * (j + 1))
                packed[0] = up if j == 0 else jnp.where(group == j, up, packed[0])
                packed[1] = down if j == 0 else jnp.where(group == j, down, packed[1])
            ys[k, t, 0, quad] = packed[0]
            ys[k, t, 1, quad] = packed[1]

    def put(t, total):
        for comp in range(24):
            acc[t, comp] = total[comp]

    def got(t):
        return [acc[t, comp] for comp in range(24)]

    def x_terms(t, field):
        f, u = field(t), link(t, 3)
        ahead = [jnp.where(x_last, roll(h, ROW - 1), roll(h, -1)) for h in project(f, 3, 1)]
        total = add_rebuilt(None, color_product(u, ahead, False), 3, 1)
        behind = color_product(u, project(f, 3, -1), True)
        behind = [jnp.where(x_first, roll(h, 1 - ROW), roll(h, 1)) for h in behind]
        put(t, add_rebuilt(total, behind, 3, -1))

    def y_terms(k, t):
        for item in y_copies(k, t):
            item.wait_recv()
        ahead, behind = [], []
        for comp in range(12):
            quad, j = comp // 4, comp % 4
            ahead.append(jnp.where(group == 3, roll(yr[k, t, 0, quad], (3 - j) * ROW), yf[k, t, comp]))
            behind.append(jnp.where(group == 0, roll(yr[k, t, 1, quad], -j * ROW), yb[k, t, comp]))
        total = add_rebuilt(got(t), color_product(link(t, 2), ahead, False), 2, 1)
        put(t, add_rebuilt(total, behind, 2, -1))

    def t_terms(k, t):
        t_copy(k, 1 - t).wait_recv()
        if t == 0:
            ahead, behind = [tf[k, 1, c] for c in range(12)], [tr[k, 1, c] for c in range(12)]
        else:
            ahead, behind = [tr[k, 0, c] for c in range(12)], [tb[k, 0, c] for c in range(12)]
        total = add_rebuilt(got(t), color_product(link(t, 0), ahead, False), 0, 1)
        put(t, add_rebuilt(total, behind, 0, -1))

    def z_terms(k, t):
        for item in z_copies(k, t):
            item.wait_recv()
        ahead = [jnp.concatenate([zf[k, t, 1, c], zr[k, t, 0, c]], axis=0) for c in range(12)]
        behind = [jnp.concatenate([zr[k, t, 1, c], zb[k, t, 0, c]], axis=0) for c in range(12)]
        total = add_rebuilt(got(t), color_product(link(t, 1), ahead, False), 1, 1)
        total = add_rebuilt(total, behind, 1, -1)
        return [spread(s_v, t, comp) + HOPPING * total[comp] for comp in range(24)]

    loads[0].wait()
    for t in range(2):
        for m in range(4):
            for entry in range(18):
                for z in range(2):
                    line = l_v[entry, m : m + 1, (2 * t + z) * LANES : (2 * t + z + 1) * LANES]
                    lb[t, m, entry, 8 * z : 8 * z + 8] = jnp.broadcast_to(line, (8, LANES))
    for load in loads[1:5]:
        load.wait()
    for t in range(2):
        prepare_z(0, t, guess_of)
        prepare_t(0, t, guess_of)
        prepare_y(0, t, guess_of)
    pl.semaphore_wait(barrier, 6)
    for item in z_copies(0, 0) + [t_copy(0, 1)] + y_copies(0, 0):
        item.start()
    for item in z_copies(0, 1) + [t_copy(0, 0)] + y_copies(0, 1):
        item.start()
    for t in range(2):
        x_terms(t, guess_of)
    for load in loads[5:]:
        load.wait()

    for t in range(2):
        y_terms(0, t)
        t_terms(0, t)
        done = z_terms(0, t)
        for comp in range(24):
            x1[t, comp] = done[comp]
        prepare_z(1, t, first_of)
        for item in z_copies(1, t):
            item.start()
        prepare_t(1, t, first_of)
        t_copy(1, t).start()
        prepare_y(1, t, first_of)
        for item in y_copies(1, t):
            item.start()
        x_terms(t, first_of)

    for t in range(2):
        y_terms(1, t)
    stores = []
    for t in range(2):
        t_terms(1, t)
        done = z_terms(1, t)
        for z in range(2):
            cell = 2 * t + z
            for comp in range(24):
                o_v[cell, pl.ds(comp, 8, stride=24), :] = done[comp][8 * z : 8 * z + 8]
            store = pltpu.make_async_copy(o_v.at[cell], o_hbm.at[:, lanes(cell)], out_sem.at[cell])
            store.start()
            stores.append(store)
    for k in range(2):
        for t in range(2):
            for item in z_copies(k, t) + [t_copy(k, t)] + y_copies(k, t):
                item.wait_send()
    for store in stores:
        store.wait()


def solution(mesh):
    y_blocks = min(8, mesh.shape["lat"] // 2)

    def on_device(sources, guess, links):
        count, parts, sites = sources.shape
        vmem, dma = pltpu.VMEM, pltpu.SemaphoreType.DMA
        anywhere = pl.BlockSpec(memory_space=pl.ANY)
        out = pl.pallas_call(
            functools.partial(kernel, y_blocks),
            out_shape=jax.ShapeDtypeStruct((count * parts, sites), F32),
            in_specs=[anywhere] * 3,
            out_specs=anywhere,
            scratch_shapes=[
                vmem((4, count * parts, LANES), F32),
                vmem((4, count * parts, LANES), F32),
                vmem((18, 4, sites), F32),
                vmem((4, count * parts, LANES), F32),
                vmem((2, 4, 18, 16, LANES), F32),
                vmem((2, 24, 16, LANES), F32),
                vmem((2, 24, 16, LANES), F32),
                vmem((2, 2, 2, 12, 8, LANES), F32),
                vmem((2, 2, 2, 12, 8, LANES), F32),
                vmem((2, 2, 2, 12, 8, LANES), F32),
                vmem((2, 2, 12, 16, LANES), F32),
                vmem((2, 2, 12, 16, LANES), F32),
                vmem((2, 2, 12, 16, LANES), F32),
                vmem((2, 2, 12, 16, LANES), F32),
                vmem((2, 2, 12, 16, LANES), F32),
                vmem((2, 2, 2, 3, 16, LANES), F32),
                vmem((2, 2, 2, 3, 16, LANES), F32),
                dma((9,)),
                dma((4,)),
                dma((2, 2, 2)),
                dma((2, 2, 2)),
                dma((2, 2)),
                dma((2, 2)),
                dma((2, 2, 2)),
                dma((2, 2, 2)),
            ],
            compiler_params=pltpu.CompilerParams(collective_id=0, has_side_effects=True),
        )(guess.reshape(count * parts, sites), sources.reshape(count * parts, sites), jnp.transpose(links, (1, 0, 2)))
        return out.reshape(sources.shape)

    spec = P(None, None, ("sub", "lat"))
    return jax.shard_map(on_device, mesh=mesh, in_specs=(spec, spec, spec), out_specs=spec, check_vma=False)
```

```python
import functools

import jax
import jax.numpy as jnp
from jax import lax
from jax.experimental import pallas as pl
from jax.experimental.pallas import tpu as pltpu
from jax.sharding import PartitionSpec as P

HOPPING = 0.125
MESH = pl.DeviceIdType.MESH
F32 = jnp.float32
ROW = 32
LANES = 128

UPPER = (
    ((0, 0), (1, 0)),
    ((0, 1), (1, 3)),
    ((1, 2), (0, 0)),
    ((1, 1), (0, 1)),
)
LOWER = (
    ((0, 0), (1, 0)),
    ((0, 3), (1, 1)),
    ((1, 0), (0, 2)),
    ((1, 3), (0, 3)),
)


def turned(pair, power):
    re, im = pair
    return (
        ((1, re), (1, im)),
        ((-1, im), (1, re)),
        ((-1, re), (-1, im)),
        ((1, im), (-1, re)),
    )[power]


def plus(value, sign, other):
    return value + other if sign > 0 else value - other


def project(f, m, parity):
    result = []
    for spin in range(2):
        half, power = UPPER[m][spin]
        for color in range(3):
            base = (spin * 3 + color) * 2
            low = ((2 + half) * 3 + color) * 2
            parts = turned((f[low], f[low + 1]), power)
            for part in range(2):
                sign, value = parts[part]
                result.append(plus(f[base + part], -parity * sign, value))
    return result


def add_rebuilt(total, h, m, parity):
    result = []
    for index in range(12):
        result.append(h[index] if total is None else total[index] + h[index])
    for spin in range(2):
        half, power = LOWER[m][spin]
        for color in range(3):
            low = (half * 3 + color) * 2
            parts = turned((h[low], h[low + 1]), power)
            for part in range(2):
                sign, value = parts[part]
                sign = -parity * sign
                place = ((2 + spin) * 3 + color) * 2 + part
                if total is None:
                    result.append(value if sign > 0 else -value)
                else:
                    result.append(plus(total[place], sign, value))
    return result


def color_product(u, h, adjoint):
    result = []
    for spin in range(2):
        for target in range(3):
            re = im = None
            for source in range(3):
                entry = (source * 3 + target if adjoint else target * 3 + source) * 2
                ur, ui = u[entry], u[entry + 1]
                vr, vi = h[(spin * 3 + source) * 2], h[(spin * 3 + source) * 2 + 1]
                if re is None:
                    re, im = ur * vr, ur * vi
                else:
                    re, im = re + ur * vr, im + ur * vi
                if adjoint:
                    re, im = re + ui * vi, im - ui * vr
                else:
                    re, im = re - ui * vi, im + ui * vr
            result.append(re)
            result.append(im)
    return result


def roll(value, shift):
    shift = shift % LANES
    return value if shift == 0 else pltpu.roll(value, shift, 1)


def kernel(
    y_blocks, g_hbm, s_hbm, l_hbm, o_ref, g_v, s_v, l_v, lb, x1, acc, zf, zb, zr, tf, tb, tr, yf, yb, ys, yr,
    in_sem, zs_sem, zr_sem, ts_sem, tr_sem, ys_sem, yr_sem,
):
    sub, lat = lax.axis_index("sub"), lax.axis_index("lat")
    n_sub, n_lat = lax.axis_size("sub"), lax.axis_size("lat")
    row, column = lat // y_blocks, lat % y_blocks
    t_up, t_down = ((sub + 1) % n_sub, lat), ((sub + n_sub - 1) % n_sub, lat)
    z_up, z_down = (sub, (lat + y_blocks) % n_lat), (sub, (lat + n_lat - y_blocks) % n_lat)
    y_up = (sub, row * y_blocks + (column + 1) % y_blocks)
    y_down = (sub, row * y_blocks + (column + y_blocks - 1) % y_blocks)

    barrier = pltpu.get_barrier_semaphore()
    for other in (z_up, z_down, t_up, t_down, y_up, y_down):
        pl.semaphore_signal(barrier, inc=1, device_id=other, device_id_type=MESH)

    def lanes(cell):
        return pl.ds(cell * LANES, LANES)

    loads = [pltpu.make_async_copy(l_hbm, l_v, in_sem.at[8])]
    for cell in range(4):
        loads.append(pltpu.make_async_copy(g_hbm.at[:, lanes(cell)], g_v.at[cell], in_sem.at[cell]))
    for cell in range(4):
        loads.append(pltpu.make_async_copy(s_hbm.at[:, lanes(cell)], s_v.at[cell], in_sem.at[4 + cell]))
    for load in loads:
        load.start()

    place = lax.broadcasted_iota(jnp.int32, (16, LANES), 1)
    x_last, x_first = place % ROW == ROW - 1, place % ROW == 0
    group = place // ROW

    def spread(ref, t, comp):
        rows = pl.ds(comp, 8, stride=24)
        return jnp.concatenate([ref[2 * t, rows, :], ref[2 * t + 1, rows, :]], axis=0)

    def guess_of(t):
        return [spread(g_v, t, comp) for comp in range(24)]

    def link(t, m):
        return [lb[t, m, entry] for entry in range(18)]

    def copy(src, dst, send, recv, other):
        return pltpu.make_async_remote_copy(
            src_ref=src, dst_ref=dst, send_sem=send, recv_sem=recv, device_id=other, device_id_type=MESH
        )

    def z_copies(k, t):
        return [
            copy(zf.at[k, t, 0], zr.at[k, t, 0], zs_sem.at[k, t, 0], zr_sem.at[k, t, 0], z_down),
            copy(zb.at[k, t, 1], zr.at[k, t, 1], zs_sem.at[k, t, 1], zr_sem.at[k, t, 1], z_up),
        ]

    def t_copy(k, t):
        src, other = (tf, t_down) if t == 0 else (tb, t_up)
        return copy(src.at[k, t], tr.at[k, t], ts_sem.at[k, t], tr_sem.at[k, t], other)

    def y_copies(k, t):
        return [
            copy(ys.at[k, t, 0], yr.at[k, t, 0], ys_sem.at[k, t, 0], yr_sem.at[k, t, 0], y_down),
            copy(ys.at[k, t, 1], yr.at[k, t, 1], ys_sem.at[k, t, 1], yr_sem.at[k, t, 1], y_up),
        ]

    def z_rows(values, z):
        return [value[8 * z : 8 * z + 8] for value in values]

    def z_link(t, z):
        return [lb[t, 1, entry, 8 * z : 8 * z + 8] for entry in range(18)]

    def prepare_z(k, t, f, ahead_of, behind_of):
        ahead = project(z_rows(f, ahead_of), 1, 1)
        behind = color_product(z_link(t, behind_of), project(z_rows(f, behind_of), 1, -1), True)
        for comp in range(12):
            zf[k, t, ahead_of, comp] = ahead[comp]
            zb[k, t, behind_of, comp] = behind[comp]

    def prepare_t(k, t, f):
        ahead = project(f, 0, 1)
        behind = color_product(link(t, 0), project(f, 0, -1), True)
        if t == 0:
            sign = jnp.where(sub == 0, -1.0, 1.0).astype(F32)
            ahead = [value * sign for value in ahead]
        else:
            sign = jnp.where(sub == n_sub - 1, -1.0, 1.0).astype(F32)
            behind = [value * sign for value in behind]
        for comp in range(12):
            tf[k, t, comp] = ahead[comp]
            tb[k, t, comp] = behind[comp]

    def prepare_y(k, t, f):
        ahead = project(f, 2, 1)
        behind = color_product(link(t, 2), project(f, 2, -1), True)
        for quad in range(3):
            packed = [None, None]
            for j in range(4):
                comp = 4 * quad + j
                up, down = roll(ahead[comp], -ROW), roll(behind[comp], ROW)
                yf[k, t, comp] = up
                yb[k, t, comp] = down
                up = up if j == 3 else roll(ahead[comp], ROW * j)
                down = down if j == 0 else roll(behind[comp], ROW * (j + 1))
                packed[0] = up if j == 0 else jnp.where(group == j, up, packed[0])
                packed[1] = down if j == 0 else jnp.where(group == j, down, packed[1])
            ys[k, t, 0, quad] = packed[0]
            ys[k, t, 1, quad] = packed[1]

    def put(t, total):
        for comp in range(24):
            acc[t, comp] = total[comp]

    def got(t):
        return [acc[t, comp] for comp in range(24)]

    def near_terms(k, t, f):
        u = link(t, 3)
        ahead = [jnp.where(x_last, roll(h, ROW - 1), roll(h, -1)) for h in project(f, 3, 1)]
        total = add_rebuilt(None, color_product(u, ahead, False), 3, 1)
        behind = color_product(u, project(f, 3, -1), True)
        behind = [jnp.where(x_first, roll(h, 1 - ROW), roll(h, 1)) for h in behind]
        total = add_rebuilt(total, behind, 3, -1)
        ahead = color_product(z_link(t, 0), [zf[k, t, 1, comp] for comp in range(12)], False)
        lower = add_rebuilt(z_rows(total, 0), ahead, 1, 1)
        upper = add_rebuilt(z_rows(total, 1), [zb[k, t, 0, comp] for comp in range(12)], 1, -1)
        put(t, [jnp.concatenate(pair, axis=0) for pair in zip(lower, upper)])

    def y_terms(k, t):
        for item in y_copies(k, t):
            item.wait_recv()
        ahead, behind = [], []
        for comp in range(12):
            quad, j = comp // 4, comp % 4
            ahead.append(jnp.where(group == 3, roll(yr[k, t, 0, quad], (3 - j) * ROW), yf[k, t, comp]))
            behind.append(jnp.where(group == 0, roll(yr[k, t, 1, quad], -j * ROW), yb[k, t, comp]))
        total = add_rebuilt(got(t), color_product(link(t, 2), ahead, False), 2, 1)
        put(t, add_rebuilt(total, behind, 2, -1))

    def t_terms(k, t):
        t_copy(k, 1 - t).wait_recv()
        if t == 0:
            ahead, behind = [tf[k, 1, c] for c in range(12)], [tr[k, 1, c] for c in range(12)]
        else:
            ahead, behind = [tr[k, 0, c] for c in range(12)], [tb[k, 0, c] for c in range(12)]
        total = add_rebuilt(got(t), color_product(link(t, 0), ahead, False), 0, 1)
        return add_rebuilt(total, behind, 0, -1)

    def far_terms(k, t):
        for item in z_copies(k, t):
            item.wait_recv()
        upper = color_product(z_link(t, 1), [zr[k, t, 0, comp] for comp in range(12)], False)
        lower = add_rebuilt(None, [zr[k, t, 1, comp] for comp in range(12)], 1, -1)
        upper = add_rebuilt(None, upper, 1, 1)
        return [jnp.concatenate(pair, axis=0) for pair in zip(lower, upper)]

    def start(*items):
        for item in items:
            item.start()

    def spread_links(m):
        for t in range(2):
            for entry in range(18):
                for z in range(2):
                    line = l_v[entry, m : m + 1, (2 * t + z) * LANES : (2 * t + z + 1) * LANES]
                    lb[t, m, entry, 8 * z : 8 * z + 8] = jnp.broadcast_to(line, (8, LANES))

    loads[0].wait()
    spread_links(1)
    for load in loads[1:5]:
        load.wait()
    prepare_z(0, 0, guess_of(0), 0, 1)
    prepare_z(0, 1, guess_of(1), 0, 1)
    pl.semaphore_wait(barrier, 6)
    start(*z_copies(0, 0))
    spread_links(0)
    prepare_t(0, 1, guess_of(1))
    prepare_t(0, 0, guess_of(0))
    start(t_copy(0, 1), t_copy(0, 0), *z_copies(0, 1))
    spread_links(2)
    for t in range(2):
        prepare_y(0, t, guess_of(t))
        start(*y_copies(0, t))
    spread_links(3)
    for t in range(2):
        prepare_z(0, t, guess_of(t), 1, 0)
        near_terms(0, t, guess_of(t))
    for load in loads[5:]:
        load.wait()

    for t in range(2):
        y_terms(0, t)
        total = t_terms(0, t)
        partial = [spread(s_v, t, comp) + HOPPING * total[comp] for comp in range(24)]
        prepare_z(1, t, partial, 0, 1)
        start(*z_copies(1, t))
        for comp in range(24):
            x1[t, comp] = partial[comp]
    for t in range(2):
        far = far_terms(0, t)
        full = [x1[t, comp] + HOPPING * far[comp] for comp in range(24)]
        prepare_t(1, t, full)
        start(t_copy(1, t))
        prepare_y(1, t, full)
        start(*y_copies(1, t))
        prepare_z(1, t, full, 1, 0)
        near_terms(1, t, full)

    for t in range(2):
        y_terms(1, t)
    for t in range(2):
        total = t_terms(1, t)
        put(t, [spread(s_v, t, comp) + HOPPING * total[comp] for comp in range(24)])
    for t in range(2):
        far = far_terms(1, t)
        done = [acc[t, comp] + HOPPING * far[comp] for comp in range(24)]
        for z in range(2):
            cell = 2 * t + z
            for comp in range(24):
                o_ref[pl.ds(comp // 8 * 32 + cell * 8 + comp % 8, 8, stride=96), :] = done[comp][8 * z : 8 * z + 8]
    for k in range(2):
        for t in range(2):
            for item in z_copies(k, t) + [t_copy(k, t)] + y_copies(k, t):
                item.wait_send()


def solution(mesh):
    y_blocks = min(8, mesh.shape["lat"] // 2)

    def on_device(sources, guess, links):
        count, parts, sites = sources.shape
        vmem, dma = pltpu.VMEM, pltpu.SemaphoreType.DMA
        anywhere = pl.BlockSpec(memory_space=pltpu.HBM)
        out = pl.pallas_call(
            functools.partial(kernel, y_blocks),
            out_shape=jax.ShapeDtypeStruct((count * parts * sites // LANES, LANES), F32),
            in_specs=[anywhere] * 3,
            out_specs=pl.BlockSpec(memory_space=pltpu.VMEM),
            scratch_shapes=[
                vmem((4, count * parts, LANES), F32),
                vmem((4, count * parts, LANES), F32),
                vmem((18, 4, sites), F32),
                vmem((2, 4, 18, 16, LANES), F32),
                vmem((2, 24, 16, LANES), F32),
                vmem((2, 24, 16, LANES), F32),
                vmem((2, 2, 2, 12, 8, LANES), F32),
                vmem((2, 2, 2, 12, 8, LANES), F32),
                vmem((2, 2, 2, 12, 8, LANES), F32),
                vmem((2, 2, 12, 16, LANES), F32),
                vmem((2, 2, 12, 16, LANES), F32),
                vmem((2, 2, 12, 16, LANES), F32),
                vmem((2, 2, 12, 16, LANES), F32),
                vmem((2, 2, 12, 16, LANES), F32),
                vmem((2, 2, 2, 3, 16, LANES), F32),
                vmem((2, 2, 2, 3, 16, LANES), F32),
                dma((9,)),
                dma((2, 2, 2)),
                dma((2, 2, 2)),
                dma((2, 2)),
                dma((2, 2)),
                dma((2, 2, 2)),
                dma((2, 2, 2)),
            ],
            compiler_params=pltpu.CompilerParams(collective_id=0, has_side_effects=True, vmem_limit_bytes=16 << 20),
        )(*[pltpu.with_memory_space_constraint(a, pltpu.HBM) for a in (guess.reshape(count * parts, sites), sources.reshape(count * parts, sites), jnp.transpose(links, (1, 0, 2)))])
        return jnp.transpose(out.reshape(count * parts // 8, sites // LANES, 8, LANES), (0, 2, 1, 3)).reshape(sources.shape)

    spec = P(None, None, ("sub", "lat"))
    return jax.shard_map(on_device, mesh=mesh, in_specs=(spec, spec, spec), out_specs=spec, check_vma=False)
```
